32 devices in a mesh: segment: 2 (over core), dp: 4 (over y, x), mp: 4 (over z).
Axes of the slice: x: 2, y: 2, z: 4, core: 2. Of those that a mesh axis runs over, the one named last changes fastest.
Arguments:
- token_ids: int32 [2, 256], replicated, may hold values from 0 to 32767
- table: bfloat16 [32768, 8192], P('dp', 'mp'), may hold values from -6 to 6
- w_up: bfloat16 [2, 8192, 32768], P('segment', 'mp', 'dp'), may hold values from -0.0625 to 0.0625
- w_down: bfloat16 [2, 32768, 8192], P('segment', 'dp', 'mp'), may hold values from -0.03125 to 0.03125
- cotangent: bfloat16 [2, 256, 8192], P(None, 'dp', 'mp'), may hold values from -6 to 6
Outputs:
- acts: bfloat16 [2, 2, 256, 8192], P('segment', None, 'dp', 'mp')
- grads: bfloat16 [2, 2, 256, 8192], P('segment', None, 'dp', 'mp')
The draws below stay inside these ranges and needn't reach their ends.
All inputs are finite; a program needn't handle non-finite values.
Results may differ from the reference program's by a relative error of at most 0.018.
Values may be sent and summed in bfloat16 or wider, within the bound.
A program may use at most 192 MiB of HBM per device.

```python
import math
import jax
import jax.numpy as jnp
import numpy as np
from jax import lax

D = 8192
FF = 32768
VOCAB = 32768
MICRO = 2
TOK_MB = 256
SEGMENTS = 2


def touch_ends(array, stream_key, smallest, top_value):
    dims = array.shape
    place = [jax.random.randint(jax.random.fold_in(stream_key, axis), (), 0, dims[axis]) for axis in range(len(dims))]
    array = array.at[tuple(place)].set(smallest)
    longest = dims.index(max(dims))
    place[longest] = (place[longest] + 1) % dims[longest]
    return array.at[tuple(place)].set(top_value)


def steps_of(key, shape, split, least, high):
    factor_of, own = 1.0, jax.random.fold_in(key, 6)
    for dim, shards_of in split:
        heights = jnp.exp(jax.random.uniform(jax.random.fold_in(own, dim), (shards_of,), jnp.float32, least / len(split), high / len(split)))
        factor_of = factor_of * jnp.repeat(heights, shape[dim] // shards_of).reshape([-1 if axis == dim else 1 for axis in range(len(shape))])
    return factor_of


def cumulative_ranks(amount, slope):
    loads = [(1 << 20) // math.isqrt(grade ** slope) + 1 for grade in range(1, amount + 1)]
    spread = 1 + sum(loads) // (1 << 30)
    return np.cumsum(np.array([max(1, weight // spread) for weight in loads]))


def ranked(rng, extent, number_of, slope):
    listing = cumulative_ranks(number_of, slope)
    pick = jax.random.randint(jax.random.fold_in(rng, 1), extent, 0, int(listing[number_of - 1]))
    standing = jnp.searchsorted(jnp.asarray(listing, jnp.int32), pick, side="right")
    return jax.random.permutation(jax.random.fold_in(rng, 2), number_of)[standing].astype(jnp.int32)


def centred(rng, shape, scale, most, shards=(), dtype=jnp.bfloat16):
    values = scale * jax.random.normal(rng, shape, jnp.float32)
    if shards:
        values = values * steps_of(rng, shape, shards, -0.22, 0.18)
    return jnp.clip(values, -most, most).astype(dtype)


def setup_inputs(seed: int = 0) -> dict:
    key_of = jax.random.split(jax.random.key(seed), 6)
    token_ids = touch_ends(ranked(key_of[0], (MICRO, TOK_MB), VOCAB, 2), jax.random.fold_in(key_of[0], 3), 0, VOCAB - 1).astype(jnp.int32)
    table = centred(key_of[1], (VOCAB, D), 1.0, 6.0, ((0, 4), (1, 4)))
    w_up = centred(key_of[2], (SEGMENTS, D, FF), D ** -0.5, 0.0625, ((0, 2), (1, 4), (2, 4)))
    w_down = centred(key_of[3], (SEGMENTS, FF, D), FF ** -0.5, 0.03125, ((0, 2), (1, 4), (2, 4)))
    cotangent = centred(key_of[4], (MICRO, TOK_MB, D), 1.0, 6.0, ((1, 4), (2, 4)))
    return dict(token_ids=token_ids, table=table, w_up=w_up, w_down=w_down, cotangent=cotangent)


root_coef = 0.7978845608028654


def gelu_value(value):
    return 0.5 * value * (1.0 + jnp.tanh(root_coef * (value + 0.044715 * value * value * value)))


def gelu_slope(value):
    inner = jnp.tanh(root_coef * (value + 0.044715 * value * value * value))
    return 0.5 * (1.0 + inner) + 0.5 * value * (1.0 - inner * inner) * root_coef * (1.0 + 0.134145 * value * value)


def section_forward(inputs, up_matrix, down_matrix):
    pre_act = jnp.dot(inputs, up_matrix, preferred_element_type=jnp.float32)
    hidden = gelu_value(pre_act).astype(jnp.bfloat16)
    mixed = jnp.dot(hidden, down_matrix, preferred_element_type=jnp.float32)
    return (inputs.astype(jnp.float32) + mixed).astype(jnp.bfloat16), pre_act


def section_backward(upstream, pre_act, up_matrix, down_matrix):
    back_hidden = lax.dot_general(upstream, down_matrix, (((1,), (1,)), ((), ())), preferred_element_type=jnp.float32)
    back_pre = (gelu_slope(pre_act) * back_hidden).astype(jnp.bfloat16)
    mixed = lax.dot_general(back_pre, up_matrix, (((1,), (1,)), ((), ())), preferred_element_type=jnp.float32)
    return (upstream.astype(jnp.float32) + mixed).astype(jnp.bfloat16)


def reference(token_ids, table, w_up, w_down, cotangent):
    first_outs, second_outs, first_grads, second_grads = [], [], [], []
    for micro_pos in range(MICRO):
        embedded = jnp.take(table, token_ids[micro_pos], axis=0)
        first_out, first_pre = section_forward(embedded, w_up[0], w_down[0])
        second_out, second_pre = section_forward(first_out, w_up[1], w_down[1])
        second_grad = section_backward(cotangent[micro_pos], second_pre, w_up[1], w_down[1])
        first_grad = section_backward(second_grad, first_pre, w_up[0], w_down[0])
        first_outs.append(first_out)
        second_outs.append(second_out)
        first_grads.append(first_grad)
        second_grads.append(second_grad)
    acts = jnp.stack([jnp.stack(first_outs), jnp.stack(second_outs)])
    grads = jnp.stack([jnp.stack(first_grads), jnp.stack(second_grads)])
    return acts, grads
```

```python
import jax
import jax.numpy as jnp
from jax import lax
from jax.sharding import PartitionSpec as P


root_coef = 0.7978845608028654


def gelu_value(value):
    return 0.5 * value * (1.0 + jnp.tanh(root_coef * (value + 0.044715 * value * value * value)))


def gelu_slope(value):
    inner = jnp.tanh(root_coef * (value + 0.044715 * value * value * value))
    return 0.5 * (1.0 + inner) + 0.5 * value * (1.0 - inner * inner) * root_coef * (
        1.0 + 0.134145 * value * value
    )


def permute_within(value, axis, segment, pairs):
    count = lax.axis_size(axis)
    offset = segment * count
    return lax.ppermute(value, ("segment", axis), [(offset + a, offset + b) for a, b in pairs])


def gather_tokens(block):
    return lax.all_gather(block, "dp", axis=block.ndim - 2, tiled=True)


def scatter_tokens(partial):
    return lax.psum_scatter(partial, "dp", scatter_dimension=partial.ndim - 2, tiled=True)


def lookup(token_ids, table):
    table_rows = table.shape[0]
    picked = token_ids - lax.axis_index("dp") * table_rows
    inside = (picked >= 0) & (picked < table_rows)
    fetched = jnp.take(table, jnp.clip(picked, 0, table_rows - 1), axis=0)
    return scatter_tokens(jnp.where(inside[..., None], fetched, jnp.zeros_like(fetched)))


def hidden_piece(weight, dim, index, count):
    size = weight.shape[dim] // count
    return lax.dynamic_slice_in_dim(weight, index * size, size, dim)


def first_half(full, weight, contract_dim, segment):
    count = lax.axis_size("mp")
    position = lax.axis_index("mp")
    parts = {}
    for k in range(count - 1, -1, -1):
        product = lax.dot_general(
            full,
            hidden_piece(weight, 1 - contract_dim, (position + k) % count, count),
            (((1,), (contract_dim,)), ((), ())),
            preferred_element_type=jnp.float32,
        )
        parts[k] = lax.optimization_barrier(product.astype(jnp.bfloat16))
    ring = [(q, (q + 1) % count) for q in range(count)]
    received = None
    for step in range(1, count):
        going = parts[count - step]
        if received is not None:
            going = (going.astype(jnp.float32) + received.astype(jnp.float32)).astype(jnp.bfloat16)
        received = permute_within(going, "mp", segment, ring)
    summed = parts[0].astype(jnp.float32)
    if received is not None:
        summed = summed + received.astype(jnp.float32)
    return summed


def second_half(inputs, active, weight, contract_dim, segment):
    count = lax.axis_size("mp")
    position = lax.axis_index("mp")
    ring = [(q, (q + 1) % count) for q in range(count)]

    def product(piece, index):
        return lax.dot_general(
            piece,
            hidden_piece(weight, contract_dim, index, count),
            (((1,), (contract_dim,)), ((), ())),
            preferred_element_type=jnp.float32,
        )

    mixed = product(active, position)
    piece = active
    for step in range(1, count):
        piece = permute_within(piece, "mp", segment, ring)
        mixed = mixed + product(piece, (position - step) % count)
    summed = scatter_tokens(mixed.astype(jnp.bfloat16))
    return (inputs.astype(jnp.float32) + summed.astype(jnp.float32)).astype(jnp.bfloat16)


def on_device(token_ids, table, w_up, w_down, cotangent):
    micro_count = cotangent.shape[0]
    up_local, down_local = w_up[0], w_down[0]
    is_first = lax.axis_index("segment") == 0
    embedded_all = lookup(token_ids, table)
    embedded_full = gather_tokens(embedded_all)
    cotangent_full = gather_tokens(cotangent)
    acts, grads = [], []
    for micro in range(micro_count):
        embedded = embedded_all[micro]
        pre_first = first_half(embedded_full[micro], up_local, 0, 0)
        first_out = second_half(embedded, gelu_value(pre_first).astype(jnp.bfloat16), down_local, 0, 0)
        handed = lax.ppermute(first_out, "segment", [(0, 1)])
        back_second = first_half(cotangent_full[micro], down_local, 1, 1)
        pre_second = first_half(gather_tokens(handed), up_local, 0, 1)
        second_grad = second_half(
            cotangent[micro], (gelu_slope(pre_second) * back_second).astype(jnp.bfloat16), up_local, 1, 1
        )
        returned = lax.ppermute(second_grad, "segment", [(1, 0)])
        second_out = second_half(handed, gelu_value(pre_second).astype(jnp.bfloat16), down_local, 0, 1)
        back_first = first_half(gather_tokens(returned), down_local, 1, 0)
        first_grad = second_half(
            returned, (gelu_slope(pre_first) * back_first).astype(jnp.bfloat16), up_local, 1, 0
        )
        acts.append(jnp.where(is_first, first_out, second_out))
        grads.append(jnp.where(is_first, first_grad, second_grad))
    return (jnp.stack(acts)[None], jnp.stack(grads)[None])


def solution(mesh):
    return jax.shard_map(
        on_device,
        mesh=mesh,
        in_specs=(
            P(),
            P("dp", "mp"),
            P("segment", "mp", "dp"),
            P("segment", "dp", "mp"),
            P(None, "dp", "mp"),
        ),
        out_specs=(P("segment", None, "dp", "mp"), P("segment", None, "dp", "mp")),
        check_vma=False,
    )
```
